512 devices in a mesh: seq: 8 (over y, core), expert: 64 (over z, x).
Axes of the slice: x: 4, y: 4, z: 16, core: 2. Of those that a mesh axis runs over, the one named last changes fastest.
Arguments:
- tokens: bfloat16 [65536, 2048], P(('seq', 'expert')), may hold values from -4 to 4
- routes: int32 [65536, 8], P(('seq', 'expert')), may hold values from 0 to 127, all different within a row; in each aligned block of 128 rows (0 to 127, 128 to 255, ...) at most 16 rows name the same one
- gate_shares: int32 [65536, 8], P(('seq', 'expert')), may hold values from 1 to 65536
- gate_up: bfloat16 [128, 2048, 768], P('expert', 'seq'), may hold values from -0.125 to 0.125
Outputs:
- gram: float32 [128, 384, 384], P('expert', 'seq')
- maxima: float32 [128, 2048], P('expert', 'seq')
The draws below stay inside these ranges and needn't reach their ends.
Inputs may be any that keep to these rules, and one draw needn't show every extreme that they name: `routes`: among the 128 rows of one device no expert is named more than 16 times.
All inputs are finite; a program needn't handle non-finite values.
Results may differ from the reference program's by a relative error of at most 0.0049.
Values may be sent and summed in bfloat16 or wider, within the bound.
A program may use at most 64 MiB of HBM per device.

```python
import math
import jax
import jax.numpy as jnp
import numpy as np
from jax import lax

D = 2048
FWIN = 384
TOP = 8
TOK_DEV = 128
EXPERTS = 128
CAP = 16
TOKENS = 65536
N_SEQ = 8
N_EXPERT = 64


def draw_tokens(key, part):
    key_base, key_chan, key_row = jax.random.split(key, 3)
    channel_scale = jnp.exp(jax.random.uniform(key_chan, (D,), jnp.float32, -1.15, 1.15))
    row_scale = jnp.exp(jax.random.uniform(key_row, (TOKENS, 1), jnp.float32, -0.5, 0.5))
    base = jax.random.normal(key_base, (TOKENS, D), jnp.float32)
    values = jnp.clip(0.5 * base * channel_scale * row_scale, -4.0, 4.0)
    return values.astype(jnp.bfloat16)


def touch_ends(array, rng, low, high):
    spot = [jax.random.randint(jax.random.fold_in(rng, axis), (), 0, length) for axis, length in enumerate(array.shape)]
    main_axis = array.shape.index(max(array.shape))
    next_to = spot[:main_axis] + [(spot[main_axis] + 1) % array.shape[main_axis]] + spot[main_axis + 1:]
    return array.at[tuple(spot)].set(low).at[tuple(next_to)].set(high)


def level_of(key, extent, cuts, least, top_value):
    factor_of = 1.0
    for position, blocks in cuts:
        heights = jax.random.uniform(jax.random.fold_in(jax.random.fold_in(key, 6), position), (blocks,), jnp.float32, least / len(cuts), top_value / len(cuts))
        factor_of = factor_of * jnp.repeat(jnp.exp(heights), extent[position] // blocks).reshape((-1,) + (1,) * (len(extent) - 1 - position))
    return factor_of


def shared_out(rng, own, number, rows, count, top, most, lean):
    order = jax.random.permutation(rng, count)
    packed, common = portions_of(count, rows * top, most, lean, True), portions_of(count, rows * top, most, lean, False)
    places = jnp.arange(count)

    def named(sizes, offset_by):
        used = int((sizes > 0).sum())
        fixed = max(1, used // 4)
        moved = fixed + (places - fixed + offset_by * (used - fixed)) % max(1, count - fixed)
        return jnp.zeros((count,), jnp.int32).at[order[jnp.where(places < fixed, places, moved)]].set(jnp.asarray(sizes, jnp.int32))

    sizes = jnp.where(number % 4 == 0, named(packed, number // 4), named(common, number - number // 4 - 1))
    mixed = jax.random.permutation(jax.random.fold_in(own, 3), count)
    donor, sink = mixed[0:count // 2 * 2:2], mixed[1:count // 2 * 2:2]
    room = jnp.minimum(sizes[donor] - 1, most - sizes[sink]) // 2
    room = jnp.where((donor == order[0]) | (sink == order[0]) | (sizes[sink] == 0), 0, jnp.maximum(room, 0))
    moved = jax.random.randint(jax.random.fold_in(own, 4), (count // 2,), 0, 1 << 20) % (room + 1)
    sizes = sizes.at[donor].add(-moved).at[sink].add(moved)
    members = jnp.searchsorted(jnp.cumsum(sizes), jnp.arange(rows * top), side="right").astype(jnp.int32)
    listing = members.reshape(top, rows).T
    listing = listing[jax.random.permutation(jax.random.fold_in(own, 1), rows)]
    offset_by = jax.random.randint(jax.random.fold_in(own, 2), (rows, 1), 0, top)
    return jnp.take_along_axis(listing, (jnp.arange(top)[None, :] + offset_by) % top, axis=1)


def portions_of(number_of, total, bound, slope, full):
    portions = [(1 << 20) // math.isqrt(rank ** slope) + 1 for rank in range(1, number_of + 1)]
    largest = bound if full else min(bound, max(-(-total // number_of), total * portions[0] // sum(portions)))
    least = 1 if total - largest >= number_of - 1 else 0
    counts, rest = [largest] + [least] * (number_of - 1), total - largest - least * (number_of - 1)
    while rest > 0:
        candidates = [i for i in range(1, number_of) if counts[i] < largest] or [i for i in range(1, number_of) if counts[i] < bound]
        whole, left = sum([portions[i] for i in candidates]), rest
        for i in candidates:
            more = min(bound - counts[i], max(1, left * portions[i] // whole), rest)
            counts[i] = counts[i] + more
            rest = rest - more
    return np.array(counts)


def noise(stream_key, dims, scale, bound, pieces=(), held_as=jnp.bfloat16):
    drawn = jax.random.normal(stream_key, dims, jnp.float32) * scale
    if len(pieces) > 0:
        drawn = level_of(stream_key, dims, pieces, -0.22, 0.18) * drawn
    return jnp.clip(drawn, min=-bound, max=bound).astype(held_as)


def setup_inputs(seed: int = 0) -> dict:
    streams_of = jax.random.split(jax.random.key(seed), 5)
    tokens = draw_tokens(jax.random.fold_in(streams_of[4], 71), 0)
    routes_keys = jax.random.split(jax.random.fold_in(streams_of[1], 1), TOKENS // TOK_DEV)
    routes_turns = jax.random.permutation(jax.random.fold_in(streams_of[1], 3), TOKENS // TOK_DEV)
    routes = jax.vmap(lambda own, number: shared_out(jax.random.fold_in(streams_of[1], 2), own, number, TOK_DEV, EXPERTS, TOP, CAP, 1))(routes_keys, routes_turns).reshape((TOKENS, TOP))
    gate_shares = touch_ends(jax.random.randint(streams_of[2], (TOKENS, TOP), 1, 65537), jax.random.fold_in(streams_of[2], 1), 1, 65536).astype(jnp.int32)
    gate_up = noise(streams_of[3], (EXPERTS, D, 2 * FWIN), D ** -0.5, 0.125, ((0, 64), (1, 8)))
    return dict(tokens=tokens, routes=routes, gate_shares=gate_shares, gate_up=gate_up)


def reference(tokens, routes, gate_shares, gate_up):
    chosen = routes.reshape(-1).astype(jnp.int32)
    shares = gate_shares.reshape(-1).astype(jnp.float32) / 65536.0
    ordering = jnp.argsort(chosen, stable=True).astype(jnp.int32)
    per_expert = jnp.bincount(chosen, length=EXPERTS).astype(jnp.int32)
    first_slot = (jnp.cumsum(per_expert) - per_expert).astype(jnp.int32)
    longest = N_SEQ * N_EXPERT * CAP
    padded_order = jnp.concatenate([ordering, jnp.zeros((longest,), jnp.int32)])
    norm_factor = EXPERTS / (TOKENS * TOP)

    def expert_stats(expert):
        pair_index = lax.dynamic_slice_in_dim(padded_order, first_slot[expert], longest)
        is_live = jnp.arange(longest, dtype=jnp.int32) < per_expert[expert]
        token_index = (pair_index // TOP).astype(jnp.int32)
        gathered = tokens[token_index]
        channel_max = jnp.max(jnp.where(is_live[:, None], jnp.abs(gathered), 0), axis=0).astype(jnp.float32)
        projected = jnp.dot(gathered, gate_up[expert], preferred_element_type=jnp.float32)
        hidden = (jax.nn.silu(projected[:, :FWIN]) * projected[:, FWIN:]).astype(jnp.bfloat16)
        pair_share = jnp.where(is_live, shares[pair_index], 0.0)
        weighted = hidden.astype(jnp.float32) * pair_share[:, None]
        weighted_high = weighted.astype(jnp.bfloat16)
        weighted_low = (weighted - weighted_high.astype(jnp.float32)).astype(jnp.bfloat16)
        gram_full = jnp.dot(hidden.T, weighted_high, preferred_element_type=jnp.float32)
        gram_full = gram_full + jnp.dot(hidden.T, weighted_low, preferred_element_type=jnp.float32)
        return gram_full * norm_factor, channel_max

    gram, maxima = lax.map(expert_stats, jnp.arange(EXPERTS, dtype=jnp.int32))
    return gram, maxima
```

```python
import functools

import jax
import jax.numpy as jnp
from jax import lax
from jax.experimental import pallas as pl
from jax.experimental.pallas import tpu as pltpu
from jax.sharding import PartitionSpec as P

NX, NY, NZ = 4, 4, 16
BLK = 128
TOP = 8
CAP = 16
D = 2048
FWIN = 384
EXPERTS = 128
HOPS = NZ // 2
HALF = BLK // 2
DSEQ = D // (2 * NY)
NB = 2 * NZ
ROWS = NB * CAP
MESH = pl.DeviceIdType.MESH
NORM = EXPERTS / (BLK * 2 * NY * NX * NZ * TOP)
F32 = jnp.float32
BF16 = jnp.bfloat16


def kernel(
    tok, meta, wgt, gram_out, max_out,
    toks, metas, picked, row_share, peak, weights, upper, proj, hid, wtd,
    part, own_part, part_max, got_x, got_x_max, slices, slice_max, got_y, got_y_max,
    loc_sem, ring_s, ring_r, rmeta_s, rmeta_r, mate_s, mate_r, mmeta_s, mmeta_r,
    swap_s, swap_r, first_s, first_r, frel_s, frel_r, sec_s, sec_r, srel_s, srel_r,
    gx_s, gx_r, mx_s, mx_r, gy_s, gy_r, my_s, my_r,
):
    seq = lax.axis_index("seq")
    exp = lax.axis_index("expert")
    y, c = seq // 2, seq % 2
    z, x = exp // NX, exp % NX
    mate_c = 1 - c

    def dev(dx=0, dy=0, dz=0, core=c):
        return ((y + dy) % NY * 2 + core, (z + dz) % NZ * NX + (x + dx) % NX)

    def send(src, dst, ss, rs, to):
        return pltpu.make_async_remote_copy(
            src_ref=src, dst_ref=dst, send_sem=ss, recv_sem=rs, device_id=to, device_id_type=MESH
        )

    barrier = pltpu.get_barrier_semaphore()
    peers = [dev(dz=1), dev(dz=-1), dev(core=mate_c)]
    peers += [dev(dx=k) for k in range(1, NX)]
    peers += [dev(dy=k, core=q) for k in range(1, NY) for q in (c, mate_c)]
    for peer in peers:
        pl.semaphore_signal(barrier, inc=1, device_id=peer, device_id_type=MESH)
    pl.semaphore_wait(barrier, len(peers))

    def origin(d, s):
        return (z - s) % NZ if d == 0 else (z + s) % NZ

    def rows_of(h):
        return pl.ds(h * HALF, HALF)

    def ring(d, s, h, o, src=None):
        there = toks.at[c, o, rows_of(h)]
        return send(there if src is None else src, there, ring_s.at[d, s, h], ring_r.at[d, s, h],
                    dev(dz=1 - 2 * d))

    def ring_meta(d, s, o, src=None):
        there = metas.at[c, o]
        return send(there if src is None else src, there, rmeta_s.at[d, s], rmeta_r.at[d, s],
                    dev(dz=1 - 2 * d))

    def mate(owner, s, d, o, part_rows=None, src=None):
        there = toks.at[owner, o] if part_rows is None else toks.at[owner, o, part_rows]
        return send(there if src is None else src, there, mate_s.at[s, d], mate_r.at[s, d],
                    dev(core=mate_c))

    def mate_meta(owner, s, d, o, src=None):
        there = metas.at[owner, o]
        return send(there if src is None else src, there, mmeta_s.at[s, d], mmeta_r.at[s, d],
                    dev(core=mate_c))

    def first_dev(step):
        return dev(dx=step * (1 - c), dy=step * c)

    def second_dev(step):
        return dev(dx=step * c, dy=step * (1 - c))

    def unit(df, ds, sl=None):
        xi = (x + df * (1 - c) + ds * c) % NX
        yi = (y + df * c + ds * (1 - c)) % NY
        if sl is None:
            return weights.at[xi, pl.ds(pl.multiple_of(yi * 2 * DSEQ, 2 * DSEQ), 2 * DSEQ)]
        return weights.at[xi, pl.ds(pl.multiple_of((yi * 2 + sl) * DSEQ, DSEQ), DSEQ)]

    def first(d, df):
        return send(unit(df, 0), unit(df, 0), first_s.at[d], first_r.at[d], first_dev(1 - 2 * d))

    def first_relay(d, df):
        return send(unit(df, 0, d), unit(df, 0, d), frel_s.at[d], frel_r.at[d],
                    first_dev(1 - 2 * d))

    def second(k, d, df, ds):
        return send(unit(df, ds), unit(df, ds), sec_s.at[k, d], sec_r.at[k, d],
                    second_dev(1 - 2 * d))

    def second_relay(k, d, df, ds):
        return send(unit(df, ds, d), unit(df, ds, d), srel_s.at[k, d], srel_r.at[k, d],
                    second_dev(1 - 2 * d))

    places = (0, -1, 1, 2)
    sides = (-1, 1)

    own_w = unit(0, 0, c)
    local = [
        pltpu.make_async_copy(tok, toks.at[c, z], loc_sem.at[0]),
        pltpu.make_async_copy(meta, metas.at[c, z], loc_sem.at[1]),
        pltpu.make_async_copy(wgt.at[c], own_w, loc_sem.at[2]),
    ]
    swap = send(wgt.at[mate_c], own_w, swap_s, swap_r, dev(core=mate_c))
    for d in (0, 1):
        ring_meta(d, 0, z, meta).start()
        for h in (0, 1):
            ring(d, 0, h, z, tok.at[rows_of(h)]).start()
    swap.start()
    for copy in local:
        copy.start()
    mate_meta(c, 0, 0, z, meta).start()
    mate(c, 0, 0, z, None, tok).start()

    lanes = lax.broadcasted_iota(jnp.int32, (BLK, BLK), 1)
    subs = lax.broadcasted_iota(jnp.int32, (BLK, BLK), 0)
    upper[...] = jnp.where(subs < lanes, 1.0, 0.0).astype(BF16)
    peak[...] = jnp.zeros_like(peak)

    local[2].wait()
    send(wgt.at[mate_c], unit(0, 0, mate_c), swap_s, swap_r, dev(core=mate_c)).wait_recv()
    for d in (0, 1):
        first(d, 0).start()
        second(0, d, 0, 0).start()

    slot = lax.broadcasted_iota(jnp.int32, (CAP, BLK), 0).astype(F32)
    expert_id = (z * 2 * NX + c + 2 * lax.broadcasted_iota(jnp.int32, (8, BLK), 0)).astype(F32)

    def pick(owner, o, b):
        info = metas[owner, o]
        named = jnp.zeros((8, BLK), F32)
        share = jnp.zeros((8, BLK), F32)
        for k in range(TOP):
            same = info[k : k + 1, :] == expert_id
            named = jnp.where(same, 1.0, named)
            share = jnp.where(same, info[TOP + k : TOP + k + 1, :], share)
        rank = jnp.dot(named.astype(BF16), upper[...], preferred_element_type=F32)
        rank = jnp.where(named > 0.5, rank, -1.0)
        at = pl.ds(pl.multiple_of(b * CAP, CAP), CAP)
        chosen = []
        for j in range(NX):
            one = jnp.where(rank[j : j + 1, :] == slot, 1.0, 0.0)
            chosen.append(one)
            col = jnp.sum(one * share[j : j + 1, :], axis=1, keepdims=True) * (1.0 / 65536.0)
            row_share[j, at, :] = jnp.broadcast_to(col, (CAP, BLK))
        chosen = jnp.concatenate(chosen, axis=0).astype(BF16)
        for n in range(0, D, 512):
            got = jnp.dot(chosen, toks[owner, o, :, n : n + 512], preferred_element_type=F32)
            picked_rows = got.astype(BF16)
            size = jnp.abs(got)
            for j in range(NX):
                picked[j, at, n : n + 512] = picked_rows[j * CAP : (j + 1) * CAP]
                both = jnp.maximum(size[j * CAP : j * CAP + 8], size[j * CAP + 8 : (j + 1) * CAP])
                peak[j, :, n : n + 512] = jnp.maximum(peak[j, :, n : n + 512], both)

    local[0].wait()
    local[1].wait()
    pick(c, z, 0)
    mate_meta(mate_c, 0, 0, z).wait_recv()
    mate(mate_c, 0, 0, z).wait_recv()
    pick(mate_c, z, 1)

    def mate_picks(s):
        for d in (0, 1):
            o = origin(d, s)
            mate_meta(mate_c, s, d, o).wait_recv()
            mate(mate_c, s, d, o).wait_recv()
            pick(mate_c, o, 4 * s + d)

    def ring_step(s, carry):
        for h in (0, 1):
            for d in (0, 1):
                o = origin(d, s)
                if h == 0:
                    ring_meta(d, s - 1, o).wait_recv()

                    @pl.when((s < HOPS - 1) | (d == 0))
                    def _():
                        ring_meta(d, s, o).start()

                    mate_meta(c, s, d, o).start()
                ring(d, s - 1, h, o).wait_recv()

                @pl.when((s < HOPS - 1) | (d == h))
                def _():
                    ring(d, s, h, o).start()

                if h == 1:
                    mate(c, s, d, o).start()

        @pl.when(s == 2)
        def _():
            for d in (0, 1):
                first(d, sides[d]).wait_recv()
                first_relay(d, sides[d]).start()
            for k in (1, 2):
                for d in (0, 1):
                    second(k, d, places[k], 0).start()

        @pl.when(s == 3)
        def _():
            for d in (0, 1):
                first_relay(d, 2).wait_recv()
                second(0, d, 0, sides[d]).wait_recv()
                second_relay(0, d, 0, sides[d]).start()
            for d in (0, 1):
                second(3, d, 2, 0).start()

        @pl.when(s == 4)
        def _():
            for k in (1, 2):
                for d in (0, 1):
                    second(k, d, places[k], sides[d]).wait_recv()
                    second_relay(k, d, places[k], sides[d]).start()

        @pl.when(s == 5)
        def _():
            for d in (0, 1):
                second(3, d, 2, sides[d]).wait_recv()
                second_relay(3, d, 2, sides[d]).start()

        for d in (0, 1):
            pick(c, origin(d, s), 4 * s - 2 + d)

        @pl.when(s >= 2)
        def _():
            mate_picks(s - 1)

        return carry

    lax.fori_loop(1, HOPS, ring_step, 0)

    far = (z + HOPS) % NZ
    last = HOPS - 1
    ring_meta(0, last, far).wait_recv()
    mate_meta(c, HOPS, 0, far).start()
    for d in (0, 1):
        ring(d, last, d, far).wait_recv()
        mate(c, HOPS, d, far, rows_of(d)).start()
    mate_picks(last)
    pick(c, far, NB - 2)
    for k in range(4):
        for d in (0, 1):
            second_relay(k, d, places[k], 2).wait_recv()
    mate_meta(mate_c, HOPS, 0, far).wait_recv()
    for d in (0, 1):
        mate(mate_c, HOPS, d, far, rows_of(d)).wait_recv()
    pick(mate_c, far, NB - 1)

    def to_x(i):
        return (
            send(part.at[i], got_x.at[i], gx_s.at[i], gx_r.at[i], dev(dx=i + 1)),
            send(part_max.at[i], got_x_max.at[i], mx_s.at[i], mx_r.at[i], dev(dx=i + 1)),
        )

    def one_expert(i, carry):
        j = (x + i + 1) % NX

        def tile(t, carry):
            m = pl.ds(pl.multiple_of((t // 3) * 256, 256), 256)
            n = pl.ds(pl.multiple_of((t % 3) * 256, 256), 256)
            proj[m, n] = jnp.dot(picked[j, m, :], weights[j, :, n], preferred_element_type=F32)
            return carry

        lax.fori_loop(0, 2 * ROWS // 512 * 3, tile, 0)

        @pl.when(i > 0)
        def _():
            for copy in to_x(i - 1):
                copy.start()

        def gate(t, carry):
            m = pl.ds(pl.multiple_of(t * 64, 64), 64)
            g = proj[m, 0:FWIN]
            h = (g / (1.0 + jnp.exp(-g)) * proj[m, FWIN : 2 * FWIN]).astype(BF16)
            s = row_share[j, m, :]
            w = h.astype(F32) * jnp.concatenate([s] * (FWIN // BLK), axis=1)
            high = w.astype(BF16)
            hid[m, :] = h
            wtd[m, 0:FWIN] = high
            wtd[m, FWIN : 2 * FWIN] = (w - high.astype(F32)).astype(BF16)
            return carry

        lax.fori_loop(0, ROWS // 64, gate, 0)
        over_rows = (((0,), (0,)), ((), ()))
        g = lax.dot_general(hid[...], wtd[:, 0:FWIN], over_rows, preferred_element_type=F32)
        g = g + lax.dot_general(
            hid[...], wtd[:, FWIN : 2 * FWIN], over_rows, preferred_element_type=F32
        )
        top = jnp.max(peak[j], axis=0, keepdims=True)
        for r in range(D // BLK):
            part_max[i, r : r + 1, :] = top[:, r * BLK : (r + 1) * BLK]

        @pl.when(i < NX - 1)
        def _():
            part[i] = g.astype(BF16)

        @pl.when(i == NX - 1)
        def _():
            own_part[...] = g

        return carry

    lax.fori_loop(0, NX, one_expert, 0)

    for i in range(NX - 1):
        for copy in to_x(i):
            copy.wait_recv()
    slice_max[...] = jnp.maximum(
        jnp.maximum(part_max[NX - 1], got_x_max[0]), jnp.maximum(got_x_max[1], got_x_max[2])
    )
    width = FWIN // (2 * NY)
    for q in range(2 * NY):
        at = pl.ds(q * width, width)
        total = own_part[at, :]
        for i in range(NX - 1):
            total = total + got_x[i, at, :].astype(F32)
        slices[q] = total.astype(BF16)
    got_y[c, y] = slices[seq]
    got_y_max[c, y] = slice_max[...]

    def to_y(k):
        dy, core = k // 2, (c if k % 2 == 0 else mate_c)
        to = dev(dy=dy, core=core)
        return (
            send(slices.at[to[0]], got_y.at[c, y], gy_s.at[k - 1], gy_r.at[k - 1], to),
            send(slice_max, got_y_max.at[c, y], my_s.at[k - 1], my_r.at[k - 1], to),
        )

    def from_y(k):
        dy, core = k // 2, (c if k % 2 == 0 else mate_c)
        src_y = (y - dy) % NY
        to = dev(dy=dy, core=core)
        return (
            send(slices.at[to[0]], got_y.at[core, src_y], gy_s.at[k - 1], gy_r.at[k - 1], to),
            send(slice_max, got_y_max.at[core, src_y], my_s.at[k - 1], my_r.at[k - 1], to),
        )

    for k in range(1, 2 * NY):
        for copy in to_y(k):
            copy.start()

    for d in (0, 1):
        first(d, 0).wait_send()
        first_relay(d, sides[d]).wait_send()
        for k in range(4):
            second(k, d, places[k], 0).wait_send()
            second_relay(k, d, places[k], sides[d]).wait_send()
    swap.wait_send()
    mate_meta(c, 0, 0, z, meta).wait_send()
    mate(c, 0, 0, z, None, tok).wait_send()
    for d in (0, 1):
        ring_meta(d, 0, z, meta).wait_send()
        for h in (0, 1):
            ring(d, 0, h, z, tok.at[rows_of(h)]).wait_send()

    def drain(s, carry):
        for d in (0, 1):
            o = origin(d, s)
            mate_meta(c, s, d, o).wait_send()
            mate(c, s, d, o).wait_send()

            @pl.when((s < HOPS - 1) | (d == 0))
            def _():
                ring_meta(d, s, o).wait_send()

            for h in (0, 1):

                @pl.when((s < HOPS - 1) | (d == h))
                def _():
                    ring(d, s, h, o).wait_send()

        return carry

    lax.fori_loop(1, HOPS, drain, 0)
    mate_meta(c, HOPS, 0, far).wait_send()
    for d in (0, 1):
        mate(c, HOPS, d, far, rows_of(d)).wait_send()
    for i in range(NX - 1):
        for copy in to_x(i):
            copy.wait_send()

    for k in range(1, 2 * NY):
        for copy in from_y(k):
            copy.wait_recv()
    row = lax.broadcasted_iota(jnp.int32, (D // BLK, BLK), 0)
    for p in (0, 1):
        total = got_y[p, 0].astype(F32)
        top = got_y_max[p, 0]
        for k in range(1, NY):
            total = total + got_y[p, k].astype(F32)
            top = jnp.maximum(top, got_y_max[p, k])
        gram_out[p] = total * NORM
        for r in (0, 1):
            here = jnp.where(row == 2 * seq + r, top, 0.0)
            max_out[p : p + 1, r * BLK : (r + 1) * BLK] = jnp.max(here, axis=0, keepdims=True)
    for k in range(1, 2 * NY):
        for copy in to_y(k):
            copy.wait_send()


def body(tokens, routes, gate_shares, gate_up):
    meta = jnp.concatenate([routes.T, gate_shares.T], axis=0).astype(F32)
    dma = pltpu.SemaphoreType.DMA
    width = FWIN // (2 * NY)
    pairs = [
        (2, HOPS, 2), (2, HOPS), (HOPS + 1, 2), (HOPS + 1, 2), (), (2,), (2,), (4, 2), (4, 2),
        (NX - 1,), (NX - 1,), (2 * NY - 1,), (2 * NY - 1,),
    ]
    sems = [dma((3,))]
    for shape in pairs:
        sems += [dma(shape), dma(shape)]
    return pl.pallas_call(
        kernel,
        out_shape=(
            jax.ShapeDtypeStruct((2, width, FWIN), F32),
            jax.ShapeDtypeStruct((2, D // (2 * NY)), F32),
        ),
        in_specs=[pl.BlockSpec(memory_space=pl.ANY)] * 3,
        out_specs=(
            pl.BlockSpec(memory_space=pltpu.VMEM),
            pl.BlockSpec(memory_space=pltpu.VMEM),
        ),
        scratch_shapes=[
            pltpu.VMEM((2, NZ, BLK, D), BF16),
            pltpu.VMEM((2, NZ, 2 * TOP, BLK), F32),
            pltpu.VMEM((NX, ROWS, D), BF16),
            pltpu.VMEM((NX, ROWS, BLK), F32),
            pltpu.VMEM((NX, 8, D), F32),
            pltpu.VMEM((NX, D, 2 * FWIN), BF16),
            pltpu.VMEM((BLK, BLK), BF16),
            pltpu.VMEM((ROWS, 2 * FWIN), F32),
            pltpu.VMEM((ROWS, FWIN), BF16),
            pltpu.VMEM((ROWS, 2 * FWIN), BF16),
            pltpu.VMEM((NX - 1, FWIN, FWIN), BF16),
            pltpu.VMEM((FWIN, FWIN), F32),
            pltpu.VMEM((NX, D // BLK, BLK), F32),
            pltpu.VMEM((NX - 1, FWIN, FWIN), BF16),
            pltpu.VMEM((NX - 1, D // BLK, BLK), F32),
            pltpu.VMEM((2 * NY, width, FWIN), BF16),
            pltpu.VMEM((D // BLK, BLK), F32),
            pltpu.VMEM((2, NY, width, FWIN), BF16),
            pltpu.VMEM((2, NY, D // BLK, BLK), F32),
            *sems,
        ],
        compiler_params=pltpu.CompilerParams(
            collective_id=0, has_side_effects=True, vmem_limit_bytes=60 * 1024 * 1024
        ),
    )(tokens, meta, gate_up)


def solution(mesh):
    return jax.shard_map(
        body,
        mesh=mesh,
        in_specs=(
            P(("seq", "expert"), None),
            P(("seq", "expert"), None),
            P(("seq", "expert"), None),
            P("expert", "seq", None),
        ),
        out_specs=(P("expert", "seq", None), P("expert", "seq")),
        check_vma=False,
    )
```

```python
import functools

import jax
import jax.numpy as jnp
from jax import lax
from jax.experimental import pallas as pl
from jax.experimental.pallas import tpu as pltpu
from jax.sharding import PartitionSpec as P

NX, NY, NZ = 4, 4, 16
BLK = 128
TOP = 8
CAP = 16
D = 2048
FWIN = 384
EXPERTS = 128
HOPS = NZ // 2
NH = 2
PIECE = BLK // NH
DSEQ = D // (2 * NY)
NB = 2 * NZ
ROWS = NB * CAP
EARLY = (256, 384)
MESH = pl.DeviceIdType.MESH
NORM = EXPERTS / (BLK * 2 * NY * NX * NZ * TOP)
F32 = jnp.float32
BF16 = jnp.bfloat16


def kernel(
    tok, routes, shares, wgt, gram_out, max_out,
    toks, metas, picked, row_share, peak, weights, upper, proj, hid, wtd,
    gram, part, part_max, got_1, got_x_max, slices, slice_max, got_2, got_y_max,
    loc_sem, ring_s, ring_r, rmeta_s, rmeta_r, mate_s, mate_r, mmeta_s, mmeta_r,
    swap_s, swap_r, first_s, first_r, frel_s, frel_r, sec_s, sec_r, srel_s, srel_r,
    g1_s, g1_r, p1_s, p1_r, mx_s, mx_r, g2_s, g2_r, my_s, my_r,
):
    seq = lax.axis_index("seq")
    exp = lax.axis_index("expert")
    y, c = seq // 2, seq % 2
    z, x = exp // NX, exp % NX
    mate_c = 1 - c

    def dev(dx=0, dy=0, dz=0, core=c):
        return ((y + dy) % NY * 2 + core, (z + dz) % NZ * NX + (x + dx) % NX)

    def send(src, dst, ss, rs, to):
        return pltpu.make_async_remote_copy(
            src_ref=src, dst_ref=dst, send_sem=ss, recv_sem=rs, device_id=to, device_id_type=MESH
        )

    barrier = pltpu.get_barrier_semaphore()
    peers = [dev(dz=1), dev(dz=-1), dev(core=mate_c)]
    peers += [dev(dx=k, core=q) for k in range(1, NX) for q in (c, mate_c)]
    peers += [dev(dy=k, core=q) for k in range(1, NY) for q in (c, mate_c)]
    for peer in peers:
        pl.semaphore_signal(barrier, inc=1, device_id=peer, device_id_type=MESH)
    own_rows = pl.ds(pl.multiple_of((y * 2 + c) * DSEQ, DSEQ), DSEQ)
    local = [
        pltpu.make_async_copy(routes, metas.at[c, z, 0:TOP], loc_sem.at[0]),
        pltpu.make_async_copy(shares, metas.at[c, z, TOP : 2 * TOP], loc_sem.at[1]),
        pltpu.make_async_copy(wgt.at[c], weights.at[x, own_rows], loc_sem.at[2]),
        pltpu.make_async_copy(tok, toks.at[c, z], loc_sem.at[3]),
    ]
    for copy in local:
        copy.start()
    lanes = lax.broadcasted_iota(jnp.int32, (BLK, BLK), 1)
    subs = lax.broadcasted_iota(jnp.int32, (BLK, BLK), 0)
    upper[...] = jnp.where(subs < lanes, 1.0, 0.0).astype(BF16)
    peak[...] = jnp.zeros_like(peak)
    pl.semaphore_wait(barrier, len(peers))

    def origin(d, s):
        return (z - s) % NZ if d == 0 else (z + s) % NZ

    def rows_of(h):
        return pl.ds(h * PIECE, PIECE)

    def ring(d, s, h, o, src=None):
        there = toks.at[c, o, rows_of(h)]
        return send(there if src is None else src, there, ring_s.at[d, s, h], ring_r.at[d, s, h],
                    dev(dz=1 - 2 * d))

    def ring_meta(d, s, o, src=None):
        there = metas.at[c, o]
        return send(there if src is None else src, there, rmeta_s.at[d, s], rmeta_r.at[d, s],
                    dev(dz=1 - 2 * d))

    def mate(owner, s, d, o, part_rows=None, src=None):
        there = toks.at[owner, o] if part_rows is None else toks.at[owner, o, part_rows]
        return send(there if src is None else src, there, mate_s.at[s, d], mate_r.at[s, d],
                    dev(core=mate_c))

    def mate_meta(owner, s, d, o, src=None):
        there = metas.at[owner, o]
        return send(there if src is None else src, there, mmeta_s.at[s, d], mmeta_r.at[s, d],
                    dev(core=mate_c))

    def first_dev(step):
        return dev(dx=step * (1 - c), dy=step * c)

    def second_dev(step):
        return dev(dx=step * c, dy=step * (1 - c))

    def unit(df, ds, sl=None):
        xi = (x + df * (1 - c) + ds * c) % NX
        yi = (y + df * c + ds * (1 - c)) % NY
        if sl is None:
            return weights.at[xi, pl.ds(pl.multiple_of(yi * 2 * DSEQ, 2 * DSEQ), 2 * DSEQ)]
        return weights.at[xi, pl.ds(pl.multiple_of((yi * 2 + sl) * DSEQ, DSEQ), DSEQ)]

    def first(d, df):
        return send(unit(df, 0), unit(df, 0), first_s.at[d], first_r.at[d], first_dev(1 - 2 * d))

    def first_relay(d, df):
        return send(unit(df, 0, d), unit(df, 0, d), frel_s.at[d], frel_r.at[d],
                    first_dev(1 - 2 * d))

    def second(k, d, df, ds):
        return send(unit(df, ds), unit(df, ds), sec_s.at[k, d], sec_r.at[k, d],
                    second_dev(1 - 2 * d))

    def second_relay(k, d, df, ds):
        return send(unit(df, ds, d), unit(df, ds, d), srel_s.at[k, d], srel_r.at[k, d],
                    second_dev(1 - 2 * d))

    places = (0, -1, 1, 2)
    sides = (-1, 1)

    swap = send(wgt.at[mate_c], weights.at[x, own_rows], swap_s, swap_r, dev(core=mate_c))
    for d in (0, 1):
        for h in range(NH):
            ring(d, 0, h, z, tok.at[rows_of(h)]).start()
    swap.start()
    local[0].wait()
    local[1].wait()
    for d in (0, 1):
        ring_meta(d, 0, z).start()
    mate_meta(c, 0, 0, z).start()
    mate(c, 0, 0, z, None, tok).start()

    local[2].wait()
    send(wgt.at[mate_c], unit(0, 0, mate_c), swap_s, swap_r, dev(core=mate_c)).wait_recv()
    for d in (0, 1):
        first(d, 0).start()
        second(0, d, 0, 0).start()

    slot = lax.broadcasted_iota(jnp.int32, (CAP, BLK), 0).astype(F32)
    expert_id = z * 2 * NX + c + 2 * lax.broadcasted_iota(jnp.int32, (8, BLK), 0)

    def pick(owner, o, b):
        info = metas[owner, o]
        named = jnp.zeros((8, BLK), F32)
        share = jnp.zeros((8, BLK), jnp.int32)
        for k in range(TOP):
            same = info[k : k + 1, :] == expert_id
            named = jnp.where(same, 1.0, named)
            share = jnp.where(same, info[TOP + k : TOP + k + 1, :], share)
        share = share.astype(F32)
        rank = jnp.dot(named.astype(BF16), upper[...], preferred_element_type=F32)
        rank = jnp.where(named > 0.5, rank, -1.0)
        at = pl.ds(pl.multiple_of(b * CAP, CAP), CAP)
        chosen = []
        for j in range(NX):
            one = jnp.where(rank[j : j + 1, :] == slot, 1.0, 0.0)
            chosen.append(one)
            col = jnp.sum(one * share[j : j + 1, :], axis=1, keepdims=True) * (1.0 / 65536.0)
            row_share[j, at, :] = jnp.broadcast_to(col, (CAP, BLK))
        chosen = jnp.concatenate(chosen, axis=0).astype(BF16)
        for n in range(0, D, 512):
            got = jnp.dot(chosen, toks[owner, o, :, n : n + 512], preferred_element_type=F32)
            picked_rows = got.astype(BF16)
            size = jnp.abs(got)
            for j in range(NX):
                picked[j, at, n : n + 512] = picked_rows[j * CAP : (j + 1) * CAP]
                both = jnp.maximum(size[j * CAP : j * CAP + 8], size[j * CAP + 8 : (j + 1) * CAP])
                peak[j, :, n : n + 512] = jnp.maximum(peak[j, :, n : n + 512], both)

    local[3].wait()
    pick(c, z, 0)
    mate_meta(mate_c, 0, 0, z).wait_recv()
    mate(mate_c, 0, 0, z).wait_recv()
    pick(mate_c, z, 1)

    over_rows = (((0,), (0,)), ((), ()))

    def project(i, start, count):
        j = (x + i + 1) % NX

        def tile(n, carry):
            n = pl.ds(pl.multiple_of(n * 256, 256), 256)
            proj[0:count, n] = jnp.dot(
                picked[j, start : start + count, :], weights[j, :, n], preferred_element_type=F32
            )
            return carry

        lax.fori_loop(0, 2 * FWIN // 256, tile, 0)

        def gate(t, carry):
            m = pl.ds(pl.multiple_of(t * 64, 64), 64)
            g = proj[m, 0:FWIN]
            h = (g / (1.0 + jnp.exp(-g)) * proj[m, FWIN : 2 * FWIN]).astype(BF16)
            s = row_share[j, pl.ds(pl.multiple_of(start + t * 64, 64), 64), :]
            w = h.astype(F32) * jnp.concatenate([s] * (FWIN // BLK), axis=1)
            high = w.astype(BF16)
            hid[m, :] = h
            wtd[m, 0:FWIN] = high
            wtd[m, FWIN : 2 * FWIN] = (w - high.astype(F32)).astype(BF16)
            return carry

        lax.fori_loop(0, count // 64, gate, 0)
        h = hid[0:count, :]
        g = lax.dot_general(h, wtd[0:count, 0:FWIN], over_rows, preferred_element_type=F32)
        g = g + lax.dot_general(
            h, wtd[0:count, FWIN : 2 * FWIN], over_rows, preferred_element_type=F32
        )
        if start == 0:
            gram[i] = g
        else:
            gram[i] = gram[i] + g

    def mate_picks(s):
        for d in (0, 1):
            o = origin(d, s)
            mate_meta(mate_c, s, d, o).wait_recv()
            mate(mate_c, s, d, o).wait_recv()
            pick(mate_c, o, 4 * s + d)

    def relayed(ks):
        for k in ks:
            for d in (0, 1):
                second_relay(k, d, places[k], 2).wait_recv()

    def ring_step(s, carry):
        for h in range(NH):
            for d in (0, 1):
                o = origin(d, s)
                if h == 0:
                    ring_meta(d, s - 1, o).wait_recv()

                    @pl.when((s < HOPS - 1) | (d == 0))
                    def _():
                        ring_meta(d, s, o).start()

                    mate_meta(c, s, d, o).start()
                ring(d, s - 1, h, o).wait_recv()

                @pl.when((s < HOPS - 1) | (d == h % 2))
                def _():
                    ring(d, s, h, o).start()

                if h == NH - 1:
                    mate(c, s, d, o).start()

            if h == 0:

                @pl.when(s >= 2)
                def _():
                    mate_picks(s - 1)

                @pl.when(s == HOPS - 2)
                def _():
                    relayed((1, 2))

                @pl.when(s == HOPS - 1)
                def _():
                    relayed((3,))

                @pl.when(s >= HOPS - 2)
                def _():
                    project(s - (HOPS - 2), 0, EARLY[0])

        @pl.when(s == 2)
        def _():
            for d in (0, 1):
                first(d, sides[d]).wait_recv()
                first_relay(d, sides[d]).start()
            for k in (1, 2):
                for d in (0, 1):
                    second(k, d, places[k], 0).start()

        @pl.when(s == 3)
        def _():
            for d in (0, 1):
                first_relay(d, 2).wait_recv()
                second(0, d, 0, sides[d]).wait_recv()
                second_relay(0, d, 0, sides[d]).start()
            for d in (0, 1):
                second(3, d, 2, 0).start()

        @pl.when(s == 4)
        def _():
            for k in (1, 2):
                for d in (0, 1):
                    second(k, d, places[k], sides[d]).wait_recv()
                    second_relay(k, d, places[k], sides[d]).start()

        @pl.when(s == 5)
        def _():
            for d in (0, 1):
                second(3, d, 2, sides[d]).wait_recv()
                second_relay(3, d, 2, sides[d]).start()

        for d in (0, 1):
            pick(c, origin(d, s), 4 * s - 2 + d)

        @pl.when(s == HOPS - 3)
        def _():
            relayed((0,))

        @pl.when((s == HOPS - 3) | (s == HOPS - 2))
        def _():
            project(HOPS - s, 0, EARLY[0])

        @pl.when(s == HOPS - 1)
        def _():
            def middle(i, carry):
                project(i, EARLY[0], EARLY[1] - EARLY[0])
                return carry

            lax.fori_loop(0, NX, middle, 0)

        return carry

    lax.fori_loop(1, HOPS, ring_step, 0)


    far = (z + HOPS) % NZ
    last = HOPS - 1
    ring_meta(0, last, far).wait_recv()
    mate_meta(c, HOPS, 0, far).start()
    for h in range(NH):
        ring(h % 2, last, h, far).wait_recv()
        mate(c, HOPS, h, far, rows_of(h)).start()
    mate_picks(last)
    pick(c, far, NB - 2)
    mate_meta(mate_c, HOPS, 0, far).wait_recv()
    for h in range(NH):
        mate(mate_c, HOPS, h, far, rows_of(h)).wait_recv()
    pick(mate_c, far, NB - 1)

    width = FWIN // (2 * NY)
    f = x * (1 - c) + y * c
    g = y * (1 - c) + x * c

    def to_x(i):
        return send(part_max.at[i], got_x_max.at[i], mx_s.at[i], mx_r.at[i], dev(dx=i + 1))

    for i in range(NX):
        top = jnp.max(peak[(x + i + 1) % NX], axis=0, keepdims=True)
        for r in range(D // BLK):
            part_max[i, r : r + 1, :] = top[:, r * BLK : (r + 1) * BLK]

    def to_1(i):
        return send(part.at[(f + i + 1) % NX], got_1.at[i], g1_s.at[i], g1_r.at[i],
                    first_dev(i + 1))

    def piece_1(i, k):
        pair = pl.ds((x + i + 1) % NX * 2, 2)
        return send(part.at[(f + k + 1) % NX, pair], got_1.at[k, pair], p1_s.at[i, k],
                    p1_r.at[i, k], first_dev(k + 1))

    def both(act, i):
        if i < NX - 1:

            @pl.when(c == 0)
            def _():
                act(to_1(i))

        @pl.when(c == 1)
        def _():
            for k in (1, 0, 2):
                act(piece_1(i, k))

    for i in range(NX):
        project(i, EARLY[1], ROWS - EARLY[1])
        if i > 0:
            both(lambda copy: copy.start(), i - 1)
        else:
            for k in range(NX - 1):
                to_x(k).start()
        j = (x + i + 1) % NX
        for q in range(2 * NY):
            piece = gram[i, q * width : (q + 1) * width, :].astype(BF16)
            part[j * (1 - c) + q // 2 * c, q * (1 - c) + (2 * j + q % 2) * c] = piece
    both(lambda copy: copy.start(), NX - 1)
    for i in range(NX - 1):
        to_x(i).wait_recv()
    slice_max[...] = jnp.maximum(
        jnp.maximum(part_max[NX - 1], got_x_max[0]), jnp.maximum(got_x_max[1], got_x_max[2])
    )
    got_y_max[c, y] = slice_max[...]
    for i in range(NX):
        both(lambda copy: copy.wait_recv(), i)
    for q in range(2 * NY):
        total = part[f, q].astype(F32)
        for i in range(NX - 1):
            total = total + got_1[i, q].astype(F32)
        slices[q] = total.astype(BF16)
    got_2[c, g] = slices[2 * g + c]

    def to_y(k):
        step, core = k // 2, (c if k % 2 == 0 else mate_c)
        here = dev(dx=step * c, dy=step * (1 - c), core=core)
        return (
            send(slices.at[2 * ((g + step) % NX) + core], got_2.at[c, g], g2_s.at[k - 1],
                 g2_r.at[k - 1], here),
            send(slice_max, got_y_max.at[c, y], my_s.at[k - 1], my_r.at[k - 1],
                 dev(dy=step, core=core)),
        )

    def from_y(k):
        step, core = k // 2, (c if k % 2 == 0 else mate_c)
        src = ((g if k % 2 == 0 else f) - step) % NX
        here = dev(dx=step * c, dy=step * (1 - c), core=core)
        return (
            send(slices.at[0], got_2.at[core, src], g2_s.at[k - 1], g2_r.at[k - 1], here),
            send(slice_max, got_y_max.at[core, (y - step) % NY], my_s.at[k - 1], my_r.at[k - 1],
                 dev(dy=step, core=core)),
        )

    for k in range(1, 2 * NY):
        for copy in to_y(k):
            copy.start()

    for d in (0, 1):
        first(d, 0).wait_send()
        first_relay(d, sides[d]).wait_send()
        for k in range(4):
            second(k, d, places[k], 0).wait_send()
            second_relay(k, d, places[k], sides[d]).wait_send()
    swap.wait_send()
    mate_meta(c, 0, 0, z).wait_send()
    mate(c, 0, 0, z, None, tok).wait_send()
    for d in (0, 1):
        ring_meta(d, 0, z).wait_send()
        for h in range(NH):
            ring(d, 0, h, z, tok.at[rows_of(h)]).wait_send()

    def drain(s, carry):
        for d in (0, 1):
            o = origin(d, s)
            mate_meta(c, s, d, o).wait_send()
            mate(c, s, d, o).wait_send()

            @pl.when((s < HOPS - 1) | (d == 0))
            def _():
                ring_meta(d, s, o).wait_send()

            for h in range(NH):

                @pl.when((s < HOPS - 1) | (d == h % 2))
                def _():
                    ring(d, s, h, o).wait_send()

        return carry

    lax.fori_loop(1, HOPS, drain, 0)
    mate_meta(c, HOPS, 0, far).wait_send()
    for h in range(NH):
        mate(c, HOPS, h, far, rows_of(h)).wait_send()
    for i in range(NX - 1):
        to_x(i).wait_send()
    for i in range(NX):
        both(lambda copy: copy.wait_send(), i)

    for k in range(1, 2 * NY):
        for copy in from_y(k):
            copy.wait_recv()
    row = lax.broadcasted_iota(jnp.int32, (D // BLK, BLK), 0)
    for p in (0, 1):
        total = got_2[p, 0].astype(F32)
        top = got_y_max[p, 0]
        for k in range(1, NY):
            total = total + got_2[p, k].astype(F32)
            top = jnp.maximum(top, got_y_max[p, k])
        gram_out[p] = total * NORM
        for r in (0, 1):
            here = jnp.where(row == 2 * seq + r, top, 0.0)
            max_out[p : p + 1, r * BLK : (r + 1) * BLK] = jnp.max(here, axis=0, keepdims=True)
    for k in range(1, 2 * NY):
        for copy in to_y(k):
            copy.wait_send()


def body(tokens, routes, gate_shares, gate_up):
    dma = pltpu.SemaphoreType.DMA
    width = FWIN // (2 * NY)
    pairs = [
        (2, HOPS, NH), (2, HOPS), (HOPS + 1, NH), (HOPS + 1, 2), (), (2,), (2,), (4, 2), (4, 2),
        (NX - 1,), (NX, NX - 1), (NX - 1,), (2 * NY - 1,), (2 * NY - 1,),
    ]
    sems = [dma((4,))]
    for shape in pairs:
        sems += [dma(shape), dma(shape)]
    return pl.pallas_call(
        kernel,
        out_shape=(
            jax.ShapeDtypeStruct((2, width, FWIN), F32),
            jax.ShapeDtypeStruct((2, D // (2 * NY)), F32),
        ),
        in_specs=[pl.BlockSpec(memory_space=pl.ANY)] * 4,
        out_specs=(
            pl.BlockSpec(memory_space=pltpu.VMEM),
            pl.BlockSpec(memory_space=pltpu.VMEM),
        ),
        scratch_shapes=[
            pltpu.VMEM((2, NZ, BLK, D), BF16),
            pltpu.VMEM((2, NZ, 2 * TOP, BLK), jnp.int32),
            pltpu.VMEM((NX, ROWS, D), BF16),
            pltpu.VMEM((NX, ROWS, BLK), F32),
            pltpu.VMEM((NX, 8, D), F32),
            pltpu.VMEM((NX, D, 2 * FWIN), BF16),
            pltpu.VMEM((BLK, BLK), BF16),
            pltpu.VMEM((EARLY[0], 2 * FWIN), F32),
            pltpu.VMEM((EARLY[0], FWIN), BF16),
            pltpu.VMEM((EARLY[0], 2 * FWIN), BF16),
            pltpu.VMEM((NX, FWIN, FWIN), F32),
            pltpu.VMEM((NX, 2 * NY, width, FWIN), BF16),
            pltpu.VMEM((NX, D // BLK, BLK), F32),
            pltpu.VMEM((NX - 1, 2 * NY, width, FWIN), BF16),
            pltpu.VMEM((NX - 1, D // BLK, BLK), F32),
            pltpu.VMEM((2 * NY, width, FWIN), BF16),
            pltpu.VMEM((D // BLK, BLK), F32),
            pltpu.VMEM((2, NY, width, FWIN), BF16),
            pltpu.VMEM((2, NY, D // BLK, BLK), F32),
            *sems,
        ],
        compiler_params=pltpu.CompilerParams(
            collective_id=0, has_side_effects=True, vmem_limit_bytes=60 * 1024 * 1024
        ),
    )(tokens, routes.T, gate_shares.T, gate_up)


def solution(mesh):
    return jax.shard_map(
        body,
        mesh=mesh,
        in_specs=(
            P(("seq", "expert"), None),
            P(("seq", "expert"), None),
            P(("seq", "expert"), None),
            P("expert", "seq", None),
        ),
        out_specs=(P("expert", "seq", None), P("expert", "seq")),
        check_vma=False,
    )
```

```python
import functools

import jax
import jax.numpy as jnp
from jax import lax
from jax.experimental import pallas as pl
from jax.experimental.pallas import tpu as pltpu
from jax.sharding import PartitionSpec as P

NX, NY, NZ = 4, 4, 16
BLK = 128
TOP = 8
CAP = 16
D = 2048
FWIN = 384
EXPERTS = 128
HOPS = NZ // 2
NH = 2
PIECE = BLK // NH
DSEQ = D // (2 * NY)
NB = 2 * NZ
ROWS = NB * CAP
EARLY = 320
MESH = pl.DeviceIdType.MESH
NORM = EXPERTS / (BLK * 2 * NY * NX * NZ * TOP)
F32 = jnp.float32
BF16 = jnp.bfloat16


def kernel(
    tok, routes, shares, wgt, gram_out, max_out,
    toks, metas, picked, row_share, peak, weights, upper, proj, hid, wtd,
    gram, part, part_max, got_1, got_x_max, slices, slice_max, got_2, got_y_max,
    loc_sem, ring_s, ring_r, rmeta_s, rmeta_r, mate_s, mate_r, mmeta_s, mmeta_r,
    swap_s, swap_r, first_s, first_r, frel_s, frel_r, sec_s, sec_r, srel_s, srel_r,
    g1_s, g1_r, p1_s, p1_r, mx_s, mx_r, g2_s, g2_r, my_s, my_r,
):
    seq = lax.axis_index("seq")
    exp = lax.axis_index("expert")
    y, c = seq // 2, seq % 2
    z, x = exp // NX, exp % NX
    mate_c = 1 - c

    def dev(dx=0, dy=0, dz=0, core=c):
        return ((y + dy) % NY * 2 + core, (z + dz) % NZ * NX + (x + dx) % NX)

    def send(src, dst, ss, rs, to):
        return pltpu.make_async_remote_copy(
            src_ref=src, dst_ref=dst, send_sem=ss, recv_sem=rs, device_id=to, device_id_type=MESH
        )

    barrier = pltpu.get_barrier_semaphore()
    peers = [dev(dz=1), dev(dz=-1), dev(core=mate_c)]
    peers += [dev(dx=k, core=q) for k in range(1, NX) for q in (c, mate_c)]
    peers += [dev(dy=k, core=q) for k in range(1, NY) for q in (c, mate_c)]
    for peer in peers:
        pl.semaphore_signal(barrier, inc=1, device_id=peer, device_id_type=MESH)
    own_rows = pl.ds(pl.multiple_of((y * 2 + c) * DSEQ, DSEQ), DSEQ)
    local = [
        pltpu.make_async_copy(routes, metas.at[c, z, 0:TOP], loc_sem.at[0]),
        pltpu.make_async_copy(shares, metas.at[c, z, TOP : 2 * TOP], loc_sem.at[1]),
        pltpu.make_async_copy(wgt.at[c], weights.at[x, own_rows], loc_sem.at[2]),
        pltpu.make_async_copy(tok, toks.at[c, z], loc_sem.at[3]),
    ]
    for copy in local:
        copy.start()
    lanes = lax.broadcasted_iota(jnp.int32, (BLK, BLK), 1)
    subs = lax.broadcasted_iota(jnp.int32, (BLK, BLK), 0)
    upper[...] = jnp.where(subs < lanes, 1.0, 0.0).astype(BF16)
    peak[...] = jnp.zeros_like(peak)
    pl.semaphore_wait(barrier, len(peers))

    def origin(d, s):
        return (z - s) % NZ if d == 0 else (z + s) % NZ

    def order(d, n):
        return n if d == 0 else NH - 1 - n

    def rows_of(h):
        return pl.ds(h * PIECE, PIECE)

    def ring(d, s, h, o, src=None):
        there = toks.at[c, o, rows_of(h)]
        return send(there if src is None else src, there, ring_s.at[d, s, h], ring_r.at[d, s, h],
                    dev(dz=1 - 2 * d))

    def ring_meta(d, s, o, src=None):
        there = metas.at[c, o]
        return send(there if src is None else src, there, rmeta_s.at[d, s], rmeta_r.at[d, s],
                    dev(dz=1 - 2 * d))

    def mate(owner, s, d, o, part_rows=None, src=None):
        there = toks.at[owner, o] if part_rows is None else toks.at[owner, o, part_rows]
        return send(there if src is None else src, there, mate_s.at[s, d], mate_r.at[s, d],
                    dev(core=mate_c))

    def mate_meta(owner, s, d, o, src=None):
        there = metas.at[owner, o]
        return send(there if src is None else src, there, mmeta_s.at[s, d], mmeta_r.at[s, d],
                    dev(core=mate_c))

    def first_dev(step):
        return dev(dx=step * (1 - c), dy=step * c)

    def second_dev(step):
        return dev(dx=step * c, dy=step * (1 - c))

    def unit(df, ds, sl=None):
        xi = (x + df * (1 - c) + ds * c) % NX
        yi = (y + df * c + ds * (1 - c)) % NY
        if sl is None:
            return weights.at[xi, pl.ds(pl.multiple_of(yi * 2 * DSEQ, 2 * DSEQ), 2 * DSEQ)]
        return weights.at[xi, pl.ds(pl.multiple_of((yi * 2 + sl) * DSEQ, DSEQ), DSEQ)]

    def first(d, df):
        return send(unit(df, 0), unit(df, 0), first_s.at[d], first_r.at[d], first_dev(1 - 2 * d))

    def first_relay(d, df):
        return send(unit(df, 0, d), unit(df, 0, d), frel_s.at[d], frel_r.at[d],
                    first_dev(1 - 2 * d))

    def second(k, d, df, ds):
        return send(unit(df, ds), unit(df, ds), sec_s.at[k, d], sec_r.at[k, d],
                    second_dev(1 - 2 * d))

    def second_relay(k, d, df, ds):
        return send(unit(df, ds, d), unit(df, ds, d), srel_s.at[k, d], srel_r.at[k, d],
                    second_dev(1 - 2 * d))

    places = (0, -1, 1, 2)
    sides = (-1, 1)

    swap = send(wgt.at[mate_c], weights.at[x, own_rows], swap_s, swap_r, dev(core=mate_c))
    for d in (0, 1):
        for n in range(NH):
            h = order(d, n)
            ring(d, 0, h, z, tok.at[rows_of(h)]).start()
    swap.start()
    local[0].wait()
    local[1].wait()
    for d in (0, 1):
        ring_meta(d, 0, z).start()
    mate_meta(c, 0, 0, z).start()
    mate(c, 0, 0, z, None, tok).start()

    local[2].wait()
    send(wgt.at[mate_c], unit(0, 0, mate_c), swap_s, swap_r, dev(core=mate_c)).wait_recv()
    for d in (0, 1):
        first(d, 0).start()
        second(0, d, 0, 0).start()

    slot = lax.broadcasted_iota(jnp.int32, (CAP, BLK), 0).astype(F32)
    expert_id = z * 2 * NX + c + 2 * lax.broadcasted_iota(jnp.int32, (8, BLK), 0)

    def slots_of(b):
        return pl.ds(b * CAP if isinstance(b, int) else pl.multiple_of(b * CAP, CAP), CAP)

    def choose(owner, o, b):
        info = metas[owner, o]
        named = jnp.zeros((8, BLK), F32)
        share = jnp.zeros((8, BLK), jnp.int32)
        for k in range(TOP):
            same = info[k : k + 1, :] == expert_id
            named = jnp.where(same, 1.0, named)
            share = jnp.where(same, info[TOP + k : TOP + k + 1, :], share)
        share = share.astype(F32)
        rank = jnp.dot(named.astype(BF16), upper[...], preferred_element_type=F32)
        rank = jnp.where(named > 0.5, rank, -1.0)
        at = slots_of(b)
        chosen = []
        for j in range(NX):
            one = jnp.where(rank[j : j + 1, :] == slot, 1.0, 0.0)
            chosen.append(one)
            col = jnp.sum(one * share[j : j + 1, :], axis=1, keepdims=True) * (1.0 / 65536.0)
            row_share[j, at, :] = jnp.broadcast_to(col, (CAP, BLK))
        return jnp.concatenate(chosen, axis=0).astype(BF16)

    def gather(chosen, owner, o, b):
        at = slots_of(b)
        for n in range(0, D, 512):
            got = jnp.dot(chosen, toks[owner, o, :, n : n + 512], preferred_element_type=F32)
            picked_rows = got.astype(BF16)
            size = jnp.abs(got)
            for j in range(NX):
                picked[j, at, n : n + 512] = picked_rows[j * CAP : (j + 1) * CAP]
                both = jnp.maximum(size[j * CAP : j * CAP + 8], size[j * CAP + 8 : (j + 1) * CAP])
                peak[j, :, n : n + 512] = jnp.maximum(peak[j, :, n : n + 512], both)

    def pick(owner, o, b):
        gather(choose(owner, o, b), owner, o, b)

    local[3].wait()
    pick(c, z, 0)
    mate_meta(mate_c, 0, 0, z).wait_recv()
    mate(mate_c, 0, 0, z).wait_recv()
    pick(mate_c, z, 1)

    def project(i, start, count, flat=False):
        j = (x + i + 1) % NX

        def loop(n, step):
            if flat:
                for t in range(n):
                    step(t, 0)
            else:
                lax.fori_loop(0, n, step, 0)

        def tile(n, carry):
            n = pl.ds(n * 256 if flat else pl.multiple_of(n * 256, 256), 256)
            proj[0:count, n] = jnp.dot(
                picked[j, start : start + count, :], weights[j, :, n], preferred_element_type=F32
            )
            return carry

        loop(2 * FWIN // 256, tile)

        def gate(t, carry):
            m = pl.ds(t * 64 if flat else pl.multiple_of(t * 64, 64), 64)
            g = proj[m, 0:FWIN]
            h = (g / (1.0 + jnp.exp(-g)) * proj[m, FWIN : 2 * FWIN]).astype(BF16)
            at = start + t * 64
            s = row_share[j, pl.ds(at if flat else pl.multiple_of(at, 64), 64), :]
            w = h.astype(F32) * jnp.concatenate([s] * (FWIN // BLK), axis=1)
            high = w.astype(BF16)
            low = count + t * 64
            hid[m, :] = h
            wtd[m, :] = high
            wtd[pl.ds(low if flat else pl.multiple_of(low, 64), 64), :] = (
                w - high.astype(F32)
            ).astype(BF16)
            return carry

        loop(count // 64, gate)
        h = hid[0:count, :].T
        g = jnp.dot(
            jnp.concatenate([h, h], axis=1), wtd[0 : 2 * count, :], preferred_element_type=F32
        )
        if start == 0:
            gram[i] = g
        else:
            gram[i] = gram[i] + g

    def mate_picks(s):
        for d in (0, 1):
            o = origin(d, s)
            mate_meta(mate_c, s, d, o).wait_recv()
            mate(mate_c, s, d, o).wait_recv()
            pick(mate_c, o, 4 * s + d)

    def relayed(ks):
        for k in ks:
            for d in (0, 1):
                second_relay(k, d, places[k], 2).wait_recv()

    def ring_step(s, carry):
        for n in range(NH):
            for d in (0, 1):
                o = origin(d, s)
                h = order(d, n)
                if n == 0:
                    ring_meta(d, s - 1, o).wait_recv()

                    @pl.when((s < HOPS - 1) | (d == 0))
                    def _():
                        ring_meta(d, s, o).start()

                    mate_meta(c, s, d, o).start()
                ring(d, s - 1, h, o).wait_recv()

                if n < NH // 2:
                    ring(d, s, h, o).start()
                else:

                    @pl.when(s < HOPS - 1)
                    def _():
                        ring(d, s, h, o).start()

                if n == NH - 1:
                    mate(c, s, d, o).start()

            if n == 0:

                @pl.when(s >= 2)
                def _():
                    mate_picks(s - 1)

                @pl.when(s == HOPS - 2)
                def _():
                    relayed((1, 2))

                @pl.when(s == HOPS - 1)
                def _():
                    relayed((3,))

                @pl.when(s >= HOPS - 2)
                def _():
                    project(s - (HOPS - 2), 0, EARLY)

        @pl.when(s == 2)
        def _():
            for d in (0, 1):
                first(d, sides[d]).wait_recv()
                first_relay(d, sides[d]).start()
            for k in (1, 2):
                for d in (0, 1):
                    second(k, d, places[k], 0).start()

        @pl.when(s == 3)
        def _():
            for d in (0, 1):
                first_relay(d, 2).wait_recv()
                second(0, d, 0, sides[d]).wait_recv()
                second_relay(0, d, 0, sides[d]).start()
            for d in (0, 1):
                second(3, d, 2, 0).start()

        @pl.when(s == 4)
        def _():
            for k in (1, 2):
                for d in (0, 1):
                    second(k, d, places[k], sides[d]).wait_recv()
                    second_relay(k, d, places[k], sides[d]).start()

        @pl.when(s == 5)
        def _():
            for d in (0, 1):
                second(3, d, 2, sides[d]).wait_recv()
                second_relay(3, d, 2, sides[d]).start()

        for d in (0, 1):
            pick(c, origin(d, s), 4 * s - 2 + d)

        @pl.when(s == HOPS - 3)
        def _():
            relayed((0,))

        @pl.when((s == HOPS - 3) | (s == HOPS - 2))
        def _():
            project(HOPS - s, 0, EARLY)

        return carry

    lax.fori_loop(1, HOPS, ring_step, 0)


    far = (z + HOPS) % NZ
    last = HOPS - 1
    mate_picks(last)
    ring_meta(0, last, far).wait_recv()
    mate_meta(c, HOPS, 0, far).start()
    own_far = choose(c, far, NB - 2)
    mate_meta(mate_c, HOPS, 0, far).wait_recv()
    mate_far = choose(mate_c, far, NB - 1)
    for n in range(NH // 2):
        for d in (0, 1):
            h = order(d, n)
            ring(d, last, h, far).wait_recv()
            mate(c, HOPS, h, far, rows_of(h)).start()
    gather(own_far, c, far, NB - 2)
    for h in range(NH):
        mate(mate_c, HOPS, h, far, rows_of(h)).wait_recv()
    gather(mate_far, mate_c, far, NB - 1)

    width = FWIN // (2 * NY)
    f = x * (1 - c) + y * c
    g = y * (1 - c) + x * c

    def to_x(i):
        return send(part_max.at[i], got_x_max.at[i], mx_s.at[i], mx_r.at[i], dev(dx=i + 1))

    for i in range(NX):
        top = jnp.max(peak[(x + i + 1) % NX], axis=0, keepdims=True)
        for r in range(D // BLK):
            part_max[i, r : r + 1, :] = top[:, r * BLK : (r + 1) * BLK]

    def to_1(i):
        return send(part.at[(f + i + 1) % NX], got_1.at[i], g1_s.at[i], g1_r.at[i],
                    first_dev(i + 1))

    def piece_1(i, k):
        pair = pl.ds((x + i + 1) % NX * 2, 2)
        return send(part.at[(f + k + 1) % NX, pair], got_1.at[k, pair], p1_s.at[i, k],
                    p1_r.at[i, k], first_dev(k + 1))

    def both(act, i):
        if i < NX - 1:

            @pl.when(c == 0)
            def _():
                act(to_1(i))

        @pl.when(c == 1)
        def _():
            for k in (1, 0, 2):
                act(piece_1(i, k))

    for i in range(NX):
        project(i, EARLY, ROWS - EARLY, flat=True)
        if i > 0:
            both(lambda copy: copy.start(), i - 1)
        else:
            for k in range(NX - 1):
                to_x(k).start()
        j = (x + i + 1) % NX
        for q in range(2 * NY):
            piece = gram[i, q * width : (q + 1) * width, :].astype(BF16)
            part[j * (1 - c) + q // 2 * c, q * (1 - c) + (2 * j + q % 2) * c] = piece
    both(lambda copy: copy.start(), NX - 1)
    for i in range(NX - 1):
        to_x(i).wait_recv()
    slice_max[...] = jnp.maximum(
        jnp.maximum(part_max[NX - 1], got_x_max[0]), jnp.maximum(got_x_max[1], got_x_max[2])
    )
    got_y_max[c, y] = slice_max[...]
    for i in range(NX):
        both(lambda copy: copy.wait_recv(), i)
    def add_up(step):
        for q in (0, 1):
            at = 2 * ((g + step) % NX) + q
            total = part[f, at].astype(F32)
            for i in range(NX - 1):
                total = total + got_1[i, at].astype(F32)
            slices[at] = total.astype(BF16)

    def to_y(k):
        step, core = k // 2, (c if k % 2 == 0 else mate_c)
        here = dev(dx=step * c, dy=step * (1 - c), core=core)
        return (
            send(slices.at[2 * ((g + step) % NX) + core], got_2.at[c, g], g2_s.at[k - 1],
                 g2_r.at[k - 1], here),
            send(slice_max, got_y_max.at[c, y], my_s.at[k - 1], my_r.at[k - 1],
                 dev(dy=step, core=core)),
        )

    def from_y(k):
        step, core = k // 2, (c if k % 2 == 0 else mate_c)
        src = ((g if k % 2 == 0 else f) - step) % NX
        here = dev(dx=step * c, dy=step * (1 - c), core=core)
        return (
            send(slices.at[0], got_2.at[core, src], g2_s.at[k - 1], g2_r.at[k - 1], here),
            send(slice_max, got_y_max.at[core, (y - step) % NY], my_s.at[k - 1], my_r.at[k - 1],
                 dev(dy=step, core=core)),
        )

    for k in range(1, 2 * NY):
        to_y(k)[1].start()
    add_up(2)
    for step in (1, 3, 0):
        add_up(step)
        before = {1: 2, 3: 1, 0: 3}[step]
        for k in (2 * before, 2 * before + 1):
            to_y(k)[0].start()
    got_2[c, g] = slices[2 * g + c]
    to_y(1)[0].start()

    for d in (0, 1):
        first(d, 0).wait_send()
        first_relay(d, sides[d]).wait_send()
        for k in range(4):
            second(k, d, places[k], 0).wait_send()
            second_relay(k, d, places[k], sides[d]).wait_send()
    swap.wait_send()
    mate_meta(c, 0, 0, z).wait_send()
    mate(c, 0, 0, z, None, tok).wait_send()
    for d in (0, 1):
        ring_meta(d, 0, z).wait_send()
        for h in range(NH):
            ring(d, 0, h, z, tok.at[rows_of(h)]).wait_send()

    def drain(s, carry):
        for d in (0, 1):
            o = origin(d, s)
            mate_meta(c, s, d, o).wait_send()
            mate(c, s, d, o).wait_send()

            @pl.when((s < HOPS - 1) | (d == 0))
            def _():
                ring_meta(d, s, o).wait_send()

            for h in range(NH):

                @pl.when((s < HOPS - 1) | (d == h // (NH // 2)))
                def _():
                    ring(d, s, h, o).wait_send()

        return carry

    lax.fori_loop(1, HOPS, drain, 0)
    mate_meta(c, HOPS, 0, far).wait_send()
    for h in range(NH):
        mate(c, HOPS, h, far, rows_of(h)).wait_send()
    for i in range(NX - 1):
        to_x(i).wait_send()
    for i in range(NX):
        both(lambda copy: copy.wait_send(), i)

    for k in range(1, 2 * NY):
        for copy in from_y(k):
            copy.wait_recv()
    row = lax.broadcasted_iota(jnp.int32, (D // BLK, BLK), 0)
    for p in (0, 1):
        total = got_2[p, 0].astype(F32)
        top = got_y_max[p, 0]
        for k in range(1, NY):
            total = total + got_2[p, k].astype(F32)
            top = jnp.maximum(top, got_y_max[p, k])
        gram_out[p] = total * NORM
        for r in (0, 1):
            here = jnp.where(row == 2 * seq + r, top, 0.0)
            max_out[p : p + 1, r * BLK : (r + 1) * BLK] = jnp.max(here, axis=0, keepdims=True)
    for k in range(1, 2 * NY):
        for copy in to_y(k):
            copy.wait_send()


def body(tokens, routes, gate_shares, gate_up):
    dma = pltpu.SemaphoreType.DMA
    width = FWIN // (2 * NY)
    pairs = [
        (2, HOPS, NH), (2, HOPS), (HOPS + 1, NH), (HOPS + 1, 2), (), (2,), (2,), (4, 2), (4, 2),
        (NX - 1,), (NX, NX - 1), (NX - 1,), (2 * NY - 1,), (2 * NY - 1,),
    ]
    sems = [dma((4,))]
    for shape in pairs:
        sems += [dma(shape), dma(shape)]
    return pl.pallas_call(
        kernel,
        out_shape=(
            jax.ShapeDtypeStruct((2, width, FWIN), F32),
            jax.ShapeDtypeStruct((2, D // (2 * NY)), F32),
        ),
        in_specs=[pl.BlockSpec(memory_space=pl.ANY)] * 4,
        out_specs=(
            pl.BlockSpec(memory_space=pltpu.VMEM),
            pl.BlockSpec(memory_space=pltpu.VMEM),
        ),
        scratch_shapes=[
            pltpu.VMEM((2, NZ, BLK, D), BF16),
            pltpu.VMEM((2, NZ, 2 * TOP, BLK), jnp.int32),
            pltpu.VMEM((NX, ROWS, D), BF16),
            pltpu.VMEM((NX, ROWS, BLK), F32),
            pltpu.VMEM((NX, 8, D), F32),
            pltpu.VMEM((NX, D, 2 * FWIN), BF16),
            pltpu.VMEM((BLK, BLK), BF16),
            pltpu.VMEM((EARLY, 2 * FWIN), F32),
            pltpu.VMEM((EARLY, FWIN), BF16),
            pltpu.VMEM((2 * EARLY, FWIN), BF16),
            pltpu.VMEM((NX, FWIN, FWIN), F32),
            pltpu.VMEM((NX, 2 * NY, width, FWIN), BF16),
            pltpu.VMEM((NX, D // BLK, BLK), F32),
            pltpu.VMEM((NX - 1, 2 * NY, width, FWIN), BF16),
            pltpu.VMEM((NX - 1, D // BLK, BLK), F32),
            pltpu.VMEM((2 * NY, width, FWIN), BF16),
            pltpu.VMEM((D // BLK, BLK), F32),
            pltpu.VMEM((2, NY, width, FWIN), BF16),
            pltpu.VMEM((2, NY, D // BLK, BLK), F32),
            *sems,
        ],
        compiler_params=pltpu.CompilerParams(
            collective_id=0, has_side_effects=True, vmem_limit_bytes=60 * 1024 * 1024
        ),
    )(tokens, routes.T, gate_shares.T, gate_up)


def solution(mesh):
    return jax.shard_map(
        body,
        mesh=mesh,
        in_specs=(
            P(("seq", "expert"), None),
            P(("seq", "expert"), None),
            P(("seq", "expert"), None),
            P("expert", "seq", None),
        ),
        out_specs=(P("expert", "seq", None), P("expert", "seq")),
        check_vma=False,
    )
```

```python
import functools

import jax
import jax.numpy as jnp
from jax import lax
from jax.experimental import pallas as pl
from jax.experimental.pallas import tpu as pltpu
from jax.sharding import PartitionSpec as P

NX, NY, NZ = 4, 4, 16
BLK = 128
TOP = 8
CAP = 16
D = 2048
FWIN = 384
EXPERTS = 128
HOPS = NZ // 2
NH = 2
PIECE = BLK // NH
DSEQ = D // (2 * NY)
NB = 2 * NZ
ROWS = NB * CAP
EARLY = 320
MESH = pl.DeviceIdType.MESH
NORM = EXPERTS / (BLK * 2 * NY * NX * NZ * TOP)
F32 = jnp.float32
BF16 = jnp.bfloat16


def kernel(
    tok, routes, shares, wgt, gram_out, max_out,
    toks, metas, picked, row_share, peak, weights, upper, proj, hid, wtd,
    gram, part, part_max, got_1, got_x_max, slices, slice_max, got_2, got_y_max,
    loc_sem, ring_s, ring_r, rmeta_s, rmeta_r, mate_s, mate_r, mmeta_s, mmeta_r,
    swap_s, swap_r, first_s, first_r, frel_s, frel_r, sec_s, sec_r, srel_s, srel_r,
    g1_s, g1_r, p1_s, p1_r, mx_s, mx_r, g2_s, g2_r, my_s, my_r,
):
    seq = lax.axis_index("seq")
    exp = lax.axis_index("expert")
    y, c = seq // 2, seq % 2
    z, x = exp // NX, exp % NX
    mate_c = 1 - c

    def dev(dx=0, dy=0, dz=0, core=c):
        return ((y + dy) % NY * 2 + core, (z + dz) % NZ * NX + (x + dx) % NX)

    def send(src, dst, ss, rs, to):
        return pltpu.make_async_remote_copy(
            src_ref=src, dst_ref=dst, send_sem=ss, recv_sem=rs, device_id=to, device_id_type=MESH
        )

    barrier = pltpu.get_barrier_semaphore()
    peers = [dev(dz=1), dev(dz=-1), dev(core=mate_c)]
    peers += [dev(dx=k, core=q) for k in range(1, NX) for q in (c, mate_c)]
    peers += [dev(dy=k, core=q) for k in range(1, NY) for q in (c, mate_c)]
    for peer in peers:
        pl.semaphore_signal(barrier, inc=1, device_id=peer, device_id_type=MESH)
    own_rows = pl.ds(pl.multiple_of((y * 2 + c) * DSEQ, DSEQ), DSEQ)
    local = [
        pltpu.make_async_copy(routes, metas.at[c, z, 0:TOP], loc_sem.at[0]),
        pltpu.make_async_copy(shares, metas.at[c, z, TOP : 2 * TOP], loc_sem.at[1]),
        pltpu.make_async_copy(wgt.at[c], weights.at[x, own_rows], loc_sem.at[2]),
        pltpu.make_async_copy(tok, toks.at[c, z], loc_sem.at[3]),
    ]
    for copy in local:
        copy.start()
    lanes = lax.broadcasted_iota(jnp.int32, (BLK, BLK), 1)
    subs = lax.broadcasted_iota(jnp.int32, (BLK, BLK), 0)
    upper[...] = jnp.where(subs < lanes, 1.0, 0.0).astype(BF16)
    peak[...] = jnp.zeros_like(peak)
    pl.semaphore_wait(barrier, len(peers))

    def origin(d, s):
        return (z - s) % NZ if d == 0 else (z + s) % NZ

    def order(d, n):
        return n if d == 0 else NH - 1 - n

    def rows_of(h):
        return pl.ds(h * PIECE, PIECE)

    def ring(d, s, h, o, src=None):
        there = toks.at[c, o, rows_of(h)]
        return send(there if src is None else src, there, ring_s.at[d, s, h], ring_r.at[d, s, h],
                    dev(dz=1 - 2 * d))

    def ring_meta(d, s, o, src=None):
        there = metas.at[c, o]
        return send(there if src is None else src, there, rmeta_s.at[d, s], rmeta_r.at[d, s],
                    dev(dz=1 - 2 * d))

    def mate(owner, s, d, o, part_rows=None, src=None):
        there = toks.at[owner, o] if part_rows is None else toks.at[owner, o, part_rows]
        return send(there if src is None else src, there, mate_s.at[s, d], mate_r.at[s, d],
                    dev(core=mate_c))

    def mate_meta(owner, s, d, o, src=None):
        there = metas.at[owner, o]
        return send(there if src is None else src, there, mmeta_s.at[s, d], mmeta_r.at[s, d],
                    dev(core=mate_c))

    def first_dev(step):
        return dev(dx=step * (1 - c), dy=step * c)

    def second_dev(step):
        return dev(dx=step * c, dy=step * (1 - c))

    def unit(df, ds, sl=None):
        xi = (x + df * (1 - c) + ds * c) % NX
        yi = (y + df * c + ds * (1 - c)) % NY
        if sl is None:
            return weights.at[xi, pl.ds(pl.multiple_of(yi * 2 * DSEQ, 2 * DSEQ), 2 * DSEQ)]
        return weights.at[xi, pl.ds(pl.multiple_of((yi * 2 + sl) * DSEQ, DSEQ), DSEQ)]

    def first(d, df):
        return send(unit(df, 0), unit(df, 0), first_s.at[d], first_r.at[d], first_dev(1 - 2 * d))

    def first_relay(d, df):
        return send(unit(df, 0, d), unit(df, 0, d), frel_s.at[d], frel_r.at[d],
                    first_dev(1 - 2 * d))

    def second(k, d, df, ds):
        return send(unit(df, ds), unit(df, ds), sec_s.at[k, d], sec_r.at[k, d],
                    second_dev(1 - 2 * d))

    def second_relay(k, d, df, ds):
        return send(unit(df, ds, d), unit(df, ds, d), srel_s.at[k, d], srel_r.at[k, d],
                    second_dev(1 - 2 * d))

    places = (0, -1, 1, 2)
    sides = (-1, 1)

    swap = send(wgt.at[mate_c], weights.at[x, own_rows], swap_s, swap_r, dev(core=mate_c))
    for d in (0, 1):
        for n in range(NH):
            h = order(d, n)
            ring(d, 0, h, z, tok.at[rows_of(h)]).start()
    swap.start()
    local[0].wait()
    local[1].wait()
    for d in (0, 1):
        ring_meta(d, 0, z).start()
    mate_meta(c, 0, 0, z).start()
    mate(c, 0, 0, z, None, tok).start()

    local[2].wait()
    send(wgt.at[mate_c], unit(0, 0, mate_c), swap_s, swap_r, dev(core=mate_c)).wait_recv()
    for d in (0, 1):
        first(d, 0).start()
        second(0, d, 0, 0).start()

    slot = lax.broadcasted_iota(jnp.int32, (CAP, BLK), 0).astype(F32)
    expert_id = z * 2 * NX + c + 2 * lax.broadcasted_iota(jnp.int32, (8, BLK), 0)

    def slots_of(b):
        return pl.ds(b * CAP if isinstance(b, int) else pl.multiple_of(b * CAP, CAP), CAP)

    def choose(owner, o, b):
        info = metas[owner, o]
        named = jnp.zeros((8, BLK), F32)
        share = jnp.zeros((8, BLK), jnp.int32)
        for k in range(TOP):
            same = info[k : k + 1, :] == expert_id
            named = jnp.where(same, 1.0, named)
            share = jnp.where(same, info[TOP + k : TOP + k + 1, :], share)
        share = share.astype(F32)
        rank = jnp.dot(named.astype(BF16), upper[...], preferred_element_type=F32)
        rank = jnp.where(named > 0.5, rank, -1.0)
        at = slots_of(b)
        chosen = []
        for j in range(NX):
            one = jnp.where(rank[j : j + 1, :] == slot, 1.0, 0.0)
            chosen.append(one)
            col = jnp.sum(one * share[j : j + 1, :], axis=1, keepdims=True) * (1.0 / 65536.0)
            row_share[j, at, :] = jnp.broadcast_to(col, (CAP, BLK))
        return jnp.concatenate(chosen, axis=0).astype(BF16)

    def gather(chosen, owner, o, b):
        at = slots_of(b)
        for n in range(0, D, 512):
            got = jnp.dot(chosen, toks[owner, o, :, n : n + 512], preferred_element_type=F32)
            picked_rows = got.astype(BF16)
            size = jnp.abs(got)
            for j in range(NX):
                picked[j, at, n : n + 512] = picked_rows[j * CAP : (j + 1) * CAP]
                both = jnp.maximum(size[j * CAP : j * CAP + 8], size[j * CAP + 8 : (j + 1) * CAP])
                peak[j, :, n : n + 512] = jnp.maximum(peak[j, :, n : n + 512], both)

    def pick(owner, o, b):
        gather(choose(owner, o, b), owner, o, b)

    local[3].wait()
    pick(c, z, 0)
    mate_meta(mate_c, 0, 0, z).wait_recv()
    mate(mate_c, 0, 0, z).wait_recv()
    pick(mate_c, z, 1)

    def project(i, start, count, flat=False):
        j = (x + i + 1) % NX

        def loop(n, step):
            if flat:
                for t in range(n):
                    step(t, 0)
            else:
                lax.fori_loop(0, n, step, 0)

        def tile(n, carry):
            n = pl.ds(n * 256 if flat else pl.multiple_of(n * 256, 256), 256)
            proj[0:count, n] = jnp.dot(
                picked[j, start : start + count, :], weights[j, :, n], preferred_element_type=F32
            )
            return carry

        loop(2 * FWIN // 256, tile)

        def gate(t, carry):
            m = pl.ds(t * 64 if flat else pl.multiple_of(t * 64, 64), 64)
            g = proj[m, 0:FWIN]
            h = (g / (1.0 + jnp.exp(-g)) * proj[m, FWIN : 2 * FWIN]).astype(BF16)
            at = start + t * 64
            s = row_share[j, pl.ds(at if flat else pl.multiple_of(at, 64), 64), :]
            w = h.astype(F32) * jnp.concatenate([s] * (FWIN // BLK), axis=1)
            high = w.astype(BF16)
            low = count + t * 64
            hid[m, :] = h
            wtd[m, :] = high
            wtd[pl.ds(low if flat else pl.multiple_of(low, 64), 64), :] = (
                w - high.astype(F32)
            ).astype(BF16)
            return carry

        loop(count // 64, gate)
        h = hid[0:count, :].T
        g = jnp.dot(
            jnp.concatenate([h, h], axis=1), wtd[0 : 2 * count, :], preferred_element_type=F32
        )
        if start == 0:
            gram[i] = g
        else:
            gram[i] = gram[i] + g

    def mate_picks(s):
        for d in (0, 1):
            o = origin(d, s)
            mate_meta(mate_c, s, d, o).wait_recv()
            mate(mate_c, s, d, o).wait_recv()
            pick(mate_c, o, 4 * s + d)

    def relayed(ks):
        for k in ks:
            for d in (0, 1):
                second_relay(k, d, places[k], 2).wait_recv()

    def ring_step(s, carry):
        for n in range(NH):
            for d in (0, 1):
                o = origin(d, s)
                h = order(d, n)
                if n == 0:
                    ring_meta(d, s - 1, o).wait_recv()

                    @pl.when((s < HOPS - 1) | (d == 0))
                    def _():
                        ring_meta(d, s, o).start()

                    mate_meta(c, s, d, o).start()
                ring(d, s - 1, h, o).wait_recv()

                if n < NH // 2:
                    ring(d, s, h, o).start()
                else:

                    @pl.when(s < HOPS - 1)
                    def _():
                        ring(d, s, h, o).start()

                if n == NH - 1:
                    mate(c, s, d, o).start()

            if n == 0:

                @pl.when(s >= 2)
                def _():
                    mate_picks(s - 1)

                @pl.when(s == HOPS - 2)
                def _():
                    relayed((1, 2))

                @pl.when(s == HOPS - 1)
                def _():
                    relayed((3,))

                @pl.when(s >= HOPS - 2)
                def _():
                    project(s - (HOPS - 2), 0, EARLY)

        @pl.when(s == 2)
        def _():
            for d in (0, 1):
                first(d, sides[d]).wait_recv()
                first_relay(d, sides[d]).start()
            for k in (1, 2):
                for d in (0, 1):
                    second(k, d, places[k], 0).start()

        @pl.when(s == 3)
        def _():
            for d in (0, 1):
                first_relay(d, 2).wait_recv()
                second(0, d, 0, sides[d]).wait_recv()
                second_relay(0, d, 0, sides[d]).start()
            for d in (0, 1):
                second(3, d, 2, 0).start()

        @pl.when(s == 4)
        def _():
            for k in (1, 2):
                for d in (0, 1):
                    second(k, d, places[k], sides[d]).wait_recv()
                    second_relay(k, d, places[k], sides[d]).start()

        @pl.when(s == 5)
        def _():
            for d in (0, 1):
                second(3, d, 2, sides[d]).wait_recv()
                second_relay(3, d, 2, sides[d]).start()

        for d in (0, 1):
            pick(c, origin(d, s), 4 * s - 2 + d)

        @pl.when(s == HOPS - 3)
        def _():
            relayed((0,))

        @pl.when((s == HOPS - 3) | (s == HOPS - 2))
        def _():
            project(HOPS - s, 0, EARLY)

        return carry

    lax.fori_loop(1, HOPS, ring_step, 0)


    far = (z + HOPS) % NZ
    last = HOPS - 1
    mate_picks(last)
    ring_meta(0, last, far).wait_recv()
    mate_meta(c, HOPS, 0, far).start()
    own_far = choose(c, far, NB - 2)
    mate_meta(mate_c, HOPS, 0, far).wait_recv()
    mate_far = choose(mate_c, far, NB - 1)
    for n in range(NH // 2):
        for d in (0, 1):
            h = order(d, n)
            ring(d, last, h, far).wait_recv()
            mate(c, HOPS, h, far, rows_of(h)).start()
    gather(own_far, c, far, NB - 2)
    for h in range(NH):
        mate(mate_c, HOPS, h, far, rows_of(h)).wait_recv()
    gather(mate_far, mate_c, far, NB - 1)

    width = FWIN // (2 * NY)
    f = x * (1 - c) + y * c
    g = y * (1 - c) + x * c

    def to_x(i):
        return send(part_max.at[i], got_x_max.at[i], mx_s.at[i], mx_r.at[i], dev(dx=i + 1))

    for i in range(NX):
        top = jnp.max(peak[(x + i + 1) % NX], axis=0, keepdims=True)
        for r in range(D // BLK):
            part_max[i, r : r + 1, :] = top[:, r * BLK : (r + 1) * BLK]

    def to_1(i):
        return send(part.at[(f + i + 1) % NX], got_1.at[i], g1_s.at[i], g1_r.at[i],
                    first_dev(i + 1))

    def piece_1(i, k):
        pair = pl.ds((x + i + 1) % NX * 2, 2)
        return send(part.at[(f + k + 1) % NX, pair], got_1.at[k, pair], p1_s.at[i, k],
                    p1_r.at[i, k], first_dev(k + 1))

    def both(act, i):
        if i < NX - 1:

            @pl.when(c == 0)
            def _():
                act(to_1(i))

        @pl.when(c == 1)
        def _():
            for k in (1, 0, 2):
                act(piece_1(i, k))

    far_first = (1, 0, 2, 3)
    for n, i in enumerate(far_first):
        project(i, EARLY, ROWS - EARLY, flat=True)
        if n > 0:
            both(lambda copy: copy.start(), far_first[n - 1])
        else:
            for k in range(NX - 1):
                to_x(k).start()
        j = (x + i + 1) % NX
        for q in range(2 * NY):
            piece = gram[i, q * width : (q + 1) * width, :].astype(BF16)
            part[j * (1 - c) + q // 2 * c, q * (1 - c) + (2 * j + q % 2) * c] = piece
    both(lambda copy: copy.start(), NX - 1)
    for i in range(NX - 1):
        to_x(i).wait_recv()
    slice_max[...] = jnp.maximum(
        jnp.maximum(part_max[NX - 1], got_x_max[0]), jnp.maximum(got_x_max[1], got_x_max[2])
    )
    got_y_max[c, y] = slice_max[...]
    for i in range(NX):
        both(lambda copy: copy.wait_recv(), i)
    def add_up(step):
        for q in (0, 1):
            at = 2 * ((g + step) % NX) + q
            total = part[f, at].astype(F32)
            for i in range(NX - 1):
                total = total + got_1[i, at].astype(F32)
            slices[at] = total.astype(BF16)

    def to_y(k):
        step, core = k // 2, (c if k % 2 == 0 else mate_c)
        here = dev(dx=step * c, dy=step * (1 - c), core=core)
        return (
            send(slices.at[2 * ((g + step) % NX) + core], got_2.at[c, g], g2_s.at[k - 1],
                 g2_r.at[k - 1], here),
            send(slice_max, got_y_max.at[c, y], my_s.at[k - 1], my_r.at[k - 1],
                 dev(dy=step, core=core)),
        )

    def from_y(k):
        step, core = k // 2, (c if k % 2 == 0 else mate_c)
        src = ((g if k % 2 == 0 else f) - step) % NX
        here = dev(dx=step * c, dy=step * (1 - c), core=core)
        return (
            send(slices.at[0], got_2.at[core, src], g2_s.at[k - 1], g2_r.at[k - 1], here),
            send(slice_max, got_y_max.at[core, (y - step) % NY], my_s.at[k - 1], my_r.at[k - 1],
                 dev(dy=step, core=core)),
        )

    for k in range(1, 2 * NY):
        to_y(k)[1].start()
    add_up(2)
    for step in (1, 3, 0):
        add_up(step)
        before = {1: 2, 3: 1, 0: 3}[step]
        for k in (2 * before, 2 * before + 1):
            to_y(k)[0].start()
    got_2[c, g] = slices[2 * g + c]
    to_y(1)[0].start()

    for d in (0, 1):
        first(d, 0).wait_send()
        first_relay(d, sides[d]).wait_send()
        for k in range(4):
            second(k, d, places[k], 0).wait_send()
            second_relay(k, d, places[k], sides[d]).wait_send()
    swap.wait_send()
    mate_meta(c, 0, 0, z).wait_send()
    mate(c, 0, 0, z, None, tok).wait_send()
    for d in (0, 1):
        ring_meta(d, 0, z).wait_send()
        for h in range(NH):
            ring(d, 0, h, z, tok.at[rows_of(h)]).wait_send()

    def drain(s, carry):
        for d in (0, 1):
            o = origin(d, s)
            mate_meta(c, s, d, o).wait_send()
            mate(c, s, d, o).wait_send()

            @pl.when((s < HOPS - 1) | (d == 0))
            def _():
                ring_meta(d, s, o).wait_send()

            for h in range(NH):

                @pl.when((s < HOPS - 1) | (d == h // (NH // 2)))
                def _():
                    ring(d, s, h, o).wait_send()

        return carry

    lax.fori_loop(1, HOPS, drain, 0)
    mate_meta(c, HOPS, 0, far).wait_send()
    for h in range(NH):
        mate(c, HOPS, h, far, rows_of(h)).wait_send()
    for i in range(NX - 1):
        to_x(i).wait_send()
    for i in range(NX):
        both(lambda copy: copy.wait_send(), i)

    for k in range(1, 2 * NY):
        for copy in from_y(k):
            copy.wait_recv()
    row = lax.broadcasted_iota(jnp.int32, (D // BLK, BLK), 0)
    for p in (0, 1):
        total = got_2[p, 0].astype(F32)
        top = got_y_max[p, 0]
        for k in range(1, NY):
            total = total + got_2[p, k].astype(F32)
            top = jnp.maximum(top, got_y_max[p, k])
        gram_out[p] = total * NORM
        for r in (0, 1):
            here = jnp.where(row == 2 * seq + r, top, 0.0)
            max_out[p : p + 1, r * BLK : (r + 1) * BLK] = jnp.max(here, axis=0, keepdims=True)
    for k in range(1, 2 * NY):
        for copy in to_y(k):
            copy.wait_send()


def body(tokens, routes, gate_shares, gate_up):
    dma = pltpu.SemaphoreType.DMA
    width = FWIN // (2 * NY)
    pairs = [
        (2, HOPS, NH), (2, HOPS), (HOPS + 1, NH), (HOPS + 1, 2), (), (2,), (2,), (4, 2), (4, 2),
        (NX - 1,), (NX, NX - 1), (NX - 1,), (2 * NY - 1,), (2 * NY - 1,),
    ]
    sems = [dma((4,))]
    for shape in pairs:
        sems += [dma(shape), dma(shape)]
    return pl.pallas_call(
        kernel,
        out_shape=(
            jax.ShapeDtypeStruct((2, width, FWIN), F32),
            jax.ShapeDtypeStruct((2, D // (2 * NY)), F32),
        ),
        in_specs=[pl.BlockSpec(memory_space=pl.ANY)] * 4,
        out_specs=(
            pl.BlockSpec(memory_space=pltpu.VMEM),
            pl.BlockSpec(memory_space=pltpu.VMEM),
        ),
        scratch_shapes=[
            pltpu.VMEM((2, NZ, BLK, D), BF16),
            pltpu.VMEM((2, NZ, 2 * TOP, BLK), jnp.int32),
            pltpu.VMEM((NX, ROWS, D), BF16),
            pltpu.VMEM((NX, ROWS, BLK), F32),
            pltpu.VMEM((NX, 8, D), F32),
            pltpu.VMEM((NX, D, 2 * FWIN), BF16),
            pltpu.VMEM((BLK, BLK), BF16),
            pltpu.VMEM((EARLY, 2 * FWIN), F32),
            pltpu.VMEM((EARLY, FWIN), BF16),
            pltpu.VMEM((2 * EARLY, FWIN), BF16),
            pltpu.VMEM((NX, FWIN, FWIN), F32),
            pltpu.VMEM((NX, 2 * NY, width, FWIN), BF16),
            pltpu.VMEM((NX, D // BLK, BLK), F32),
            pltpu.VMEM((NX - 1, 2 * NY, width, FWIN), BF16),
            pltpu.VMEM((NX - 1, D // BLK, BLK), F32),
            pltpu.VMEM((2 * NY, width, FWIN), BF16),
            pltpu.VMEM((D // BLK, BLK), F32),
            pltpu.VMEM((2, NY, width, FWIN), BF16),
            pltpu.VMEM((2, NY, D // BLK, BLK), F32),
            *sems,
        ],
        compiler_params=pltpu.CompilerParams(
            collective_id=0, has_side_effects=True, vmem_limit_bytes=60 * 1024 * 1024
        ),
    )(tokens, routes.T, gate_shares.T, gate_up)


def solution(mesh):
    return jax.shard_map(
        body,
        mesh=mesh,
        in_specs=(
            P(("seq", "expert"), None),
            P(("seq", "expert"), None),
            P(("seq", "expert"), None),
            P("expert", "seq", None),
        ),
        out_specs=(P("expert", "seq", None), P("expert", "seq")),
        check_vma=False,
    )
```
